32 devices in a mesh: layer: 8 (over z, x), row: 4 (over y, core).
Axes of the slice: x: 2, y: 2, z: 4, core: 2. Of those that a mesh axis runs over, the one named last changes fastest.
Arguments:
- leaf_rhs: bfloat16 [32768, 512], P(('layer', 'row')), may hold values from -3 to 3
- leaf_inv: bfloat16 [256, 128, 128], P(('layer', 'row')), may hold values from -1 to 1.25, as said below
- coupling: bfloat16 [32768, 3, 256], P(('layer', 'row')), may hold values from -0.09375 to 0.09375
- pattern: int32 [256, 3], P(('layer', 'row')), may hold values 0 or 1
- anc_rhs: float32 [8, 3, 1024, 512], P('layer', None, 'row'), may hold values from -2 to 2
- anc_blocks: bfloat16 [8, 6, 1024, 1024], P('layer', None, 'row'), may hold values from -1 to 1.25, as said below
Outputs:
- x_leaf: float32 [32768, 512], P(('layer', 'row'))
- x_anc: float32 [8, 3, 1024, 512], P('layer', None, 'row')
The draws below stay inside these ranges and needn't reach their ends.
Inputs may be any that keep to these rules, and one draw needn't show every extreme that they name: `leaf_inv`: each block is lower triangular with a positive diagonal. For every level t and block index k of blk(s, t), the copies anc_blocks[l, k] are equal for all layers l of one group of 2 ** (t + 1) layers; the blocks blk(t, t) are lower triangular with a positive diagonal.
All inputs are finite; a program needn't handle non-finite values. No bound on the sum of `pattern` on one device may be relied on, other than what follows from the above.
Results may differ from the reference program's by a relative error of at most 0.009.
Values may be sent and summed in bfloat16 or wider, within the bound.
A program may use at most 64 MiB of HBM per device.

```python
import math
import jax
import jax.numpy as jnp
from jax import lax

B = 128
R = 512
ANC = 1024
SN_DEV = 8
LEVELS = 3
ANC_DEV = 256
LEAF_SN = 256
LEAF_ROWS = 32768
N_LAYER = 8
N_ROW = 4


def lower_inverse(key, block_count, block_order):
    key_diagonal, key_lower = jax.random.split(key)
    row_ids = jnp.arange(block_order)[:, None]
    column_ids = jnp.arange(block_order)[None, :]
    below_mask = (row_ids > column_ids).astype(jnp.float32)
    diagonal_part = jax.random.uniform(key_diagonal, (block_count, block_order), jnp.float32, 0.6, 1.2)
    lower_part = jnp.clip(jax.random.normal(key_lower, (block_count, block_order, block_order), jnp.float32), -4.0, 4.0)
    lower_part = lower_part * (0.5 / math.sqrt(block_order * 1.0)) * below_mask
    return lower_part + diagonal_part[:, :, None] * jnp.eye(block_order, dtype=jnp.float32)


def draw_leaf_inv(key, part):
    return lower_inverse(jax.random.fold_in(key, 11), LEAF_SN, B).astype(jnp.bfloat16)


def draw_anc_blocks(key, part):
    layer_total = 2 ** LEVELS
    blocks_out = []
    for tree_level in range(LEVELS):
        group_size = 2 ** (tree_level + 1)
        group_count = layer_total // group_size
        for above in range(tree_level, LEVELS):
            sub_key = jax.random.fold_in(jax.random.fold_in(key, 31 + tree_level), above)
            if above == tree_level:
                fresh = lower_inverse(sub_key, group_count, ANC)
            else:
                scale_value = 0.6 / math.sqrt(ANC * 2.0 ** (above - tree_level))
                fresh = jnp.clip(jax.random.normal(sub_key, (group_count, ANC, ANC), jnp.float32), -4.0, 4.0) * scale_value
            blocks_out.append(jnp.repeat(fresh.astype(jnp.bfloat16), group_size, axis=0))
    return jnp.stack(blocks_out, axis=1)


def draw_anc_rhs(key, part):
    sub_key = jax.random.fold_in(key, 57)
    shape_full = (2 ** LEVELS, LEVELS, ANC, R)
    scales = 0.5 * 2.0 ** (-(jnp.arange(LEVELS, dtype=jnp.float32) + 1.0) / 2.0)
    base_values = jnp.clip(jax.random.normal(sub_key, shape_full, jnp.float32), -4.0, 4.0)
    return base_values * scales[None, :, None, None]


def touch_ends(result, own_key, low, high):
    extent = result.shape
    spot = [jax.random.randint(jax.random.fold_in(own_key, axis), (), 0, extent[axis]) for axis in range(len(extent))]
    result = result.at[tuple(spot)].set(low)
    longest = extent.index(max(extent))
    spot[longest] = (spot[longest] + 1) % extent[longest]
    return result.at[tuple(spot)].set(high)


def block_levels(key, shape, shards, smallest, largest):
    loudness, own = 1.0, jax.random.fold_in(key, 6)
    for axis_at, parts in shards:
        heights = jnp.exp(jax.random.uniform(jax.random.fold_in(own, axis_at), (parts,), jnp.float32, smallest / len(shards), largest / len(shards)))
        loudness = loudness * jnp.repeat(heights, shape[axis_at] // parts).reshape([-1 if axis == axis_at else 1 for axis in range(len(shape))])
    return loudness


def scatter_about(own_key, extent, deviation, most, shards=(), kind=jnp.bfloat16):
    entries = deviation * jax.random.normal(own_key, extent, jnp.float32)
    if shards:
        entries = entries * block_levels(own_key, extent, shards, -0.22, 0.18)
    return jnp.clip(entries, -most, most).astype(kind)


def setup_inputs(seed: int = 0) -> dict:
    key_of = jax.random.split(jax.random.key(seed), 7)
    leaf_rhs = scatter_about(key_of[0], (LEAF_ROWS, R), 0.5, 3.0, ((0, 32),))
    leaf_inv = draw_leaf_inv(jax.random.fold_in(key_of[6], 71), 0)
    coupling = scatter_about(key_of[2], (LEAF_ROWS, LEVELS, ANC_DEV), (SN_DEV * B * N_LAYER // 2) ** -0.5, 0.09375, ((0, 32),))
    pattern = touch_ends((jax.random.randint(key_of[3], (LEAF_SN, LEVELS), 0, 4) < 3).astype(jnp.int32), jax.random.fold_in(key_of[3], 1), 0, 1)
    anc_rhs = draw_anc_rhs(jax.random.fold_in(key_of[6], 71), 0)
    anc_blocks = draw_anc_blocks(jax.random.fold_in(key_of[6], 71), 0)
    return dict(leaf_rhs=leaf_rhs, leaf_inv=leaf_inv, coupling=coupling, pattern=pattern, anc_rhs=anc_rhs, anc_blocks=anc_blocks)


def block_start(tree_level, level_total):
    return tree_level * level_total - tree_level * (tree_level - 1) // 2


def reference(leaf_rhs, leaf_inv, coupling, pattern, anc_rhs, anc_blocks):
    devices = N_LAYER * N_ROW
    rows_dev = SN_DEV * B
    right_dev = leaf_rhs.reshape(devices, SN_DEV, B, R)
    inverse_dev = leaf_inv.reshape(devices, SN_DEV, B, B)
    coupling_dev = coupling.reshape(devices, SN_DEV, B, LEVELS, ANC_DEV)
    pattern_dev = pattern.reshape(devices, SN_DEV, LEVELS)

    def masked_of(coupling_one, pattern_one):
        scaled = coupling_one * pattern_one.astype(jnp.bfloat16)[:, None, :, None]
        return scaled.reshape(rows_dev, LEVELS * ANC_DEV)

    def forward_leaf(operands):
        right_side, inverse, coupling_one, pattern_one = operands
        leaf_y = jnp.einsum("kab,kbr->kar", inverse.astype(jnp.float32), right_side.astype(jnp.float32))
        leaf_yb = leaf_y.astype(jnp.bfloat16).reshape(rows_dev, R)
        masked = masked_of(coupling_one, pattern_one)
        leaf_terms = jnp.dot(masked.T, leaf_yb, preferred_element_type=jnp.float32)
        return leaf_y, leaf_terms.reshape(LEVELS, ANC_DEV, R)

    leaf_y, leaf_terms = lax.map(forward_leaf, (right_dev, inverse_dev, coupling_dev, pattern_dev))
    leaf_terms = leaf_terms.reshape(N_LAYER, N_ROW, LEVELS, ANC_DEV, R)
    leaf_terms = leaf_terms.transpose(0, 2, 1, 3, 4).reshape(N_LAYER, LEVELS, ANC, R)
    share = anc_rhs - leaf_terms
    lowered = jnp.zeros((N_LAYER, LEVELS, ANC, R), jnp.float32)
    y_list = []
    for tree_level in range(LEVELS):
        group_size = 2 ** (tree_level + 1)
        group_count = N_LAYER // group_size
        level_total = (share[:, tree_level] - lowered[:, tree_level]).reshape(group_count, group_size, ANC, R).sum(axis=1)
        z_level = level_total.astype(jnp.bfloat16)
        first_block = block_start(tree_level, LEVELS)
        blocks = anc_blocks[::group_size, first_block:first_block + LEVELS - tree_level].astype(jnp.float32)
        product = jnp.einsum("gkab,gbr->gkar", blocks, z_level.astype(jnp.float32))
        y_list.append(product[:, 0].astype(jnp.bfloat16))
        for above in range(tree_level + 1, LEVELS):
            lowered = lowered.at[::group_size, above].add(product[:, above - tree_level])
    answers = [None] * LEVELS
    for tree_level in reversed(range(LEVELS)):
        group_size = 2 ** (tree_level + 1)
        first_block = block_start(tree_level, LEVELS)
        blocks = anc_blocks[::group_size, first_block:first_block + LEVELS - tree_level].astype(jnp.float32)
        pieces_list = [y_list[tree_level]]
        for above in range(tree_level + 1, LEVELS):
            pieces_list.append(-jnp.repeat(answers[above].astype(jnp.bfloat16), 2 ** (above - tree_level), axis=0))
        stacked_vals = jnp.stack(pieces_list, axis=1).astype(jnp.float32)
        answers[tree_level] = jnp.einsum("gkab,gkar->gbr", blocks, stacked_vals)
    x_anc = jnp.stack([jnp.repeat(answers[tree_level], 2 ** (tree_level + 1), axis=0) for tree_level in range(LEVELS)], axis=1)
    solved_bf = x_anc.astype(jnp.bfloat16).reshape(N_LAYER, LEVELS, N_ROW, ANC_DEV, R)
    solved_bf = solved_bf.transpose(0, 2, 1, 3, 4).reshape(devices, LEVELS * ANC_DEV, R)

    def backward_leaf(operands):
        leaf_one, inverse, coupling_one, pattern_one, solved_one = operands
        masked = masked_of(coupling_one, pattern_one)
        back_terms = jnp.dot(masked, solved_one, preferred_element_type=jnp.float32)
        leaf_vb = (leaf_one.reshape(rows_dev, R) - back_terms).astype(jnp.bfloat16)
        return jnp.einsum("kba,kbr->kar", inverse.astype(jnp.float32), leaf_vb.reshape(SN_DEV, B, R).astype(jnp.float32))

    x_leaf = lax.map(backward_leaf, (leaf_y, inverse_dev, coupling_dev, pattern_dev, solved_bf))
    return x_leaf.reshape(LEAF_ROWS, R), x_anc
```

```python
import functools

import jax
import jax.numpy as jnp
from jax import lax
from jax.experimental import pallas as pl
from jax.experimental.pallas import tpu as pltpu
from jax.sharding import PartitionSpec as P

MESH = pl.DeviceIdType.MESH
LANES = 128


def block_start(tree_level, level_total):
    return tree_level * level_total - tree_level * (tree_level - 1) // 2


def plan(levels, cols):
    widths, splits, width = [], [], cols
    for _ in range(levels):
        split = width % (2 * LANES) == 0
        width = width // 2 if split else width
        widths.append(width)
        splits.append(split)
    return widths, splits


def tdot(a, b):
    return lax.dot_general(a, b, (((0,), (0,)), ((), ())), preferred_element_type=jnp.float32)


def dot(a, b):
    return jnp.dot(a, b, preferred_element_type=jnp.float32)


class Copies:
    def __init__(self, send, recv):
        self.send, self.recv, self.count, self.all = send, recv, 0, []

    def start(self, src, dst, device):
        copy = pltpu.make_async_remote_copy(
            src_ref=src,
            dst_ref=dst,
            send_sem=self.send.at[self.count],
            recv_sem=self.recv.at[self.count],
            device_id=device,
            device_id_type=MESH,
        )
        copy.start()
        self.count += 1
        self.all.append(copy)
        return copy


def copies_needed(levels, n_row, splits):
    half = n_row // 2
    total = 0
    for t in range(levels):
        total += 2
        total += 1 + 2 * (half - 1)
        total += half + half - 1
        total += (levels - t) if splits[t] else 0
    return total


def separators(dims, share, anc, out, refs):
    levels, n_row, rows, cols = dims
    widths, splits = plan(levels, cols)
    half = n_row // 2
    tx, rx, pend, zs, acc, ps, pr, qs, qr, wide, send, recv = refs
    lay = lax.axis_index("layer")
    row = lax.axis_index("row")
    core = lax.rem(row, 2)
    yy = row // 2
    mate = {"row": yy * 2 + (1 - core)}
    bits = [lax.rem(lay // 2**t, 2) for t in range(levels)]
    across = [{"layer": lay + (1 - 2 * bits[t]) * 2**t} for t in range(levels)]

    barrier = pltpu.get_barrier_semaphore()
    for t in range(levels):
        pl.semaphore_signal(barrier, inc=1, device_id=across[t], device_id_type=MESH)
    for i in range(1, n_row):
        pl.semaphore_signal(
            barrier, inc=1, device_id={"row": lax.rem(row + i, n_row)}, device_id_type=MESH
        )
    pl.semaphore_wait(barrier, levels + n_row - 1)
    copies = Copies(send, recv)

    def piece(t, which):
        return pl.ds(pl.multiple_of(which * widths[t], LANES), widths[t])

    def offer(t, source):
        for s in range(t, levels):
            if splits[t]:
                value = source(s, piece(t, 1 - bits[t]))
            else:
                value = source(s, slice(None))
            tx[t][s - t] = value.astype(jnp.bfloat16)
            if s == t:
                first = copies.start(tx[t].at[pl.ds(0, 1)], rx[t].at[pl.ds(0, 1)], across[t])
        rest = None
        if levels - t > 1:
            later = pl.ds(1, levels - t - 1)
            rest = copies.start(tx[t].at[later], rx[t].at[later], across[t])
        return first, rest

    def source_share(s, part):
        return share[s, :, part]

    source = source_share
    flight = offer(0, source)
    later_work = None
    for t in range(levels):
        own = piece(t, bits[t]) if splits[t] else slice(None)
        if later_work is not None:
            later_work()
        flight[0].wait_recv()
        zs[t][row] = (source(t, own) + rx[t][0].astype(jnp.float32)).astype(jnp.bfloat16)
        gathers = []
        for i in range(1, half):
            other = lax.rem(yy + i, half) * 2 + core
            gathers.append(copies.start(zs[t].at[row], zs[t].at[row], {"row": other}))
        to_mate = copies.start(zs[t].at[row], zs[t].at[row], mate)
        if flight[1] is not None:
            flight[1].wait_recv()
        first_block = block_start(t, levels)
        above = levels - t - 1

        def sums_of(slot, t=t, first_block=first_block, above=above):
            column = pl.ds(pl.multiple_of(slot * rows, LANES), rows)
            return [dot(anc[first_block + 1 + k, :, column], zs[t][slot]) for k in range(above)]

        def add(old, new):
            return [a + b for a, b in zip(old, new)]

        total = sums_of(row)
        to_mate.wait_recv()
        total = add(total, sums_of(yy * 2 + 1 - core))
        passed = []
        for i in range(1, half):
            gathers[i - 1].wait_recv()
            origin = lax.rem(yy - i + half, half) * 2
            passed.append(copies.start(zs[t].at[origin + core], zs[t].at[origin + core], mate))
            total = add(total, sums_of(origin + core))
        for i in range(1, half):
            passed[i - 1].wait_recv()
            origin = lax.rem(yy - i + half, half) * 2
            total = add(total, sums_of(origin + 1 - core))
        for k in range(above):
            pend[t][k] = source(t + 1 + k, own) + rx[t][1 + k].astype(jnp.float32) - total[k]

        def source_pend(s, part, t=t):
            return pend[t][s - t - 1, :, part]

        source = source_pend
        if t + 1 < levels:
            flight = offer(t + 1, source)

        def later_work(t=t, first_block=first_block):
            z_all = zs[t][...].reshape(n_row * rows, widths[t])
            y_here = dot(anc[first_block], z_all).astype(jnp.bfloat16)
            for other in range(n_row):
                acc[t][other] = tdot(anc[first_block, :, other * rows : (other + 1) * rows], y_here)

    later_work()
    at = {}
    for t in reversed(range(levels)):
        first_block = block_start(t, levels)
        mine = piece(t, bits[t])
        widening = {}
        for s in range(t + 1, levels):
            if splits[t]:
                wider = wide[s][t]
                wider[:, mine] = at[s][...]
                widening[s] = copies.start(wider.at[:, mine], wider.at[:, mine], across[t])

        def part_of(dest, t=t, first_block=first_block):
            column = pl.ds(pl.multiple_of(dest * rows, LANES), rows)
            value = acc[t][dest]
            for s in range(t + 1, levels):
                value = value - tdot(anc[first_block + s - t, :, column], at[s][...])
            return value

        first_stage = []
        order = list(range(1, half)) + [0]
        for i in order:
            dest = lax.rem(yy + i, half) * 2 + 1 - core
            ps[t][i] = part_of(dest).astype(jnp.bfloat16)
            first_stage.append(copies.start(ps[t].at[i], pr[t].at[i], mate))
        second_stage = []
        for n, i in enumerate(order[:-1]):
            dest = lax.rem(yy + i, half) * 2 + core
            value = part_of(dest)
            first_stage[n].wait_recv()
            qs[t][i - 1] = (value + pr[t][i].astype(jnp.float32)).astype(jnp.bfloat16)
            second_stage.append(copies.start(qs[t].at[i - 1], qr[t].at[i - 1], {"row": dest}))
        value = part_of(row)
        first_stage[-1].wait_recv()
        value = value + pr[t][0].astype(jnp.float32)
        for n, i in enumerate(order[:-1]):
            second_stage[n].wait_recv()
            value = value + qr[t][i - 1].astype(jnp.float32)
        rounded = value.astype(jnp.bfloat16)
        wider = wide[t][t]
        if splits[t]:
            wider[:, mine] = rounded
            widening[t] = copies.start(wider.at[:, mine], wider.at[:, mine], across[t])
        else:
            wider[...] = rounded
        for s in range(t, levels):
            if splits[t]:
                widening[s].wait_recv()
                at[s] = wide[s][t]
            elif s == t:
                at[s] = wider
    for s in range(levels):
        out[s] = at[s][...]
    for copy in copies.all:
        copy.wait_send()


def kernel(dims, counts, share, anc, out, *scratch):
    refs, used = [], 0
    for count in counts:
        refs.append(scratch[used : used + count])
        used += count
    levels = dims[0]
    wide_flat = refs[-1]
    wide, used_wide = [], 0
    for s in range(levels):
        wide.append(wide_flat[used_wide : used_wide + s + 1])
        used_wide += s + 1
    send, recv = scratch[used:]
    separators(dims, share, anc, out, (*refs[:-1], wide, send, recv))


def solve_separators(share, anc):
    levels, rows, cols = share.shape
    n_row = lax.axis_size("row")
    half = n_row // 2
    widths, splits = plan(levels, cols)
    outer = [cols] + widths[:-1]
    span = range(levels)
    bf, f32 = jnp.bfloat16, jnp.float32
    groups = [
        [pltpu.VMEM((levels - t, rows, widths[t]), bf) for t in span],
        [pltpu.VMEM((levels - t, rows, widths[t]), bf) for t in span],
        [pltpu.VMEM((max(levels - t - 1, 1), rows, widths[t]), f32) for t in span],
        [pltpu.VMEM((n_row, rows, widths[t]), bf) for t in span],
        [pltpu.VMEM((n_row, rows, widths[t]), f32) for t in span],
        [pltpu.VMEM((half, rows, widths[t]), bf) for t in span],
        [pltpu.VMEM((half, rows, widths[t]), bf) for t in span],
        [pltpu.VMEM((max(half - 1, 1), rows, widths[t]), bf) for t in span],
        [pltpu.VMEM((max(half - 1, 1), rows, widths[t]), bf) for t in span],
        [pltpu.VMEM((rows, outer[t]), bf) for s in span for t in range(s + 1)],
    ]
    total = copies_needed(levels, n_row, splits)
    scratch = [ref for group in groups for ref in group]
    scratch += [pltpu.SemaphoreType.DMA((total,)), pltpu.SemaphoreType.DMA((total,))]
    return pl.pallas_call(
        functools.partial(kernel, (levels, n_row, rows, cols), [len(g) for g in groups]),
        out_shape=jax.ShapeDtypeStruct((levels, rows, cols), bf),
        in_specs=[pl.BlockSpec(memory_space=pltpu.VMEM)] * 2,
        out_specs=pl.BlockSpec(memory_space=pltpu.VMEM),
        scratch_shapes=scratch,
        compiler_params=pltpu.CompilerParams(collective_id=0, has_side_effects=True),
        name="separators",
    )(share, anc)


def body(leaf_rhs, leaf_inv, coupling, pattern, anc_rhs, anc_blocks):
    levels_here = anc_rhs.shape[1]
    supers = leaf_inv.shape[0]
    block_width = leaf_inv.shape[1]
    num_sides = leaf_rhs.shape[1]
    sep_rows = anc_rhs.shape[2]
    leaf_rows = supers * block_width
    leaf_y = jnp.einsum(
        "kab,kbr->kar",
        leaf_inv,
        leaf_rhs.reshape(supers, block_width, num_sides),
        preferred_element_type=jnp.float32,
    )
    leaf_yb = leaf_y.astype(jnp.bfloat16).reshape(leaf_rows, num_sides)
    masked = (
        coupling.reshape(supers, block_width, levels_here, sep_rows)
        * pattern.astype(jnp.bfloat16)[:, None, :, None]
    )
    masked = masked.reshape(leaf_rows, levels_here * sep_rows)
    leaf_terms = tdot(masked, leaf_yb)
    share = anc_rhs[0] - leaf_terms.reshape(levels_here, sep_rows, num_sides)
    solved = solve_separators(share, anc_blocks[0])
    solved_bf = solved.reshape(levels_here * sep_rows, num_sides)
    anc_out = solved.astype(jnp.float32)
    back_terms = dot(masked, solved_bf)
    leaf_vb = (leaf_y.reshape(leaf_rows, num_sides) - back_terms).astype(jnp.bfloat16)
    x_leaf = jnp.einsum(
        "kba,kbr->kar",
        leaf_inv,
        leaf_vb.reshape(supers, block_width, num_sides),
        preferred_element_type=jnp.float32,
    )
    return (x_leaf.reshape(leaf_rows, num_sides), anc_out[None])


def solution(mesh):
    placed = (
        P(("layer", "row"), None),
        P(("layer", "row"), None, None),
        P(("layer", "row"), None, None),
        P(("layer", "row"), None),
        P("layer", None, "row", None),
        P("layer", None, "row", None),
    )
    return jax.shard_map(
        body,
        mesh=mesh,
        in_specs=placed,
        out_specs=(P(("layer", "row"), None), P("layer", None, "row", None)),
        check_vma=False,
    )
```

```python
import functools

import jax
import jax.numpy as jnp
from jax import lax
from jax.experimental import pallas as pl
from jax.experimental.pallas import tpu as pltpu
from jax.sharding import PartitionSpec as P

MESH = pl.DeviceIdType.MESH
LANES = 128
BF, F32 = jnp.bfloat16, jnp.float32


def block_start(tree_level, level_total):
    return tree_level * level_total - tree_level * (tree_level - 1) // 2


def plan(levels, cols):
    counts, splits, count = [], [], cols // LANES
    for _ in range(levels):
        split = count % 2 == 0
        count = count // 2 if split else count
        counts.append(count)
        splits.append(split)
    return counts, splits


def tdot(a, b):
    return lax.dot_general(a, b, (((0,), (0,)), ((), ())), preferred_element_type=F32)


def dot(a, b):
    return jnp.dot(a, b, preferred_element_type=F32)


class Copies:
    def __init__(self, send, recv):
        self.send, self.recv, self.count, self.all = send, recv, 0, []

    def start(self, src, dst, device):
        copy = pltpu.make_async_remote_copy(
            src_ref=src,
            dst_ref=dst,
            send_sem=self.send.at[self.count],
            recv_sem=self.recv.at[self.count],
            device_id=device,
            device_id_type=MESH,
        )
        copy.start()
        self.count += 1
        self.all.append(copy)
        return copy


def copies_needed(levels, n_row, counts, splits):
    half = n_row // 2
    total = 0
    for t in range(levels):
        each = 2 + 1 + 2 * (half - 1) + half + half - 1
        each += (levels - t) if splits[t] else 0
        total += each * counts[t]
    return total


def kernel(dims, rhs_in, inv_in, coup_in, pat, ancr_in, anc_in, leaf_out, out, *scratch):
    levels, n_row, blocks, supers, width = dims
    rhs, inv, coup, ancr, anc, ly, yb, mk, mt, atr, pend, wide = scratch[:12]
    used = 12
    groups = []
    for _ in range(8):
        groups.append(scratch[used : used + levels])
        used += levels
    tx, rx, zs, acc, ps, pr, qs, qr = groups
    send, recv, local = scratch[used:]
    counts, splits = plan(levels, blocks * LANES)
    rows = anc.shape[1]
    half = n_row // 2
    lay = lax.axis_index("layer")
    row = lax.axis_index("row")
    core = lax.rem(row, 2)
    yy = row // 2
    mate = {"row": yy * 2 + (1 - core)}
    bits = [lax.rem(lay // 2**t, 2) for t in range(levels)]
    across = [{"layer": lay + (1 - 2 * bits[t]) * 2**t} for t in range(levels)]

    loads = []
    for n, (src, dst) in enumerate(
        [(rhs_in, rhs), (inv_in, inv)]
        + [(coup_in.at[s], coup.at[s]) for s in range(levels)]
        + [(ancr_in, ancr), (anc_in, anc)]
    ):
        load = pltpu.make_async_copy(src, dst, local.at[n])
        load.start()
        loads.append(load)

    barrier = pltpu.get_barrier_semaphore()
    for t in range(levels):
        pl.semaphore_signal(barrier, inc=1, device_id=across[t], device_id_type=MESH)
    for i in range(1, n_row):
        pl.semaphore_signal(
            barrier, inc=1, device_id={"row": lax.rem(row + i, n_row)}, device_id_type=MESH
        )
    copies = Copies(send, recv)

    order = list(range(counts[-1]))
    for t in reversed(range(levels)):
        if splits[t]:
            near = [bits[t] * counts[t] + j for j in order]
            order = [(1 - bits[t]) * counts[t] + j for j in order] + near
    columns = [pl.ds(pl.multiple_of(j * LANES, LANES), LANES) for j in order]

    def own(t):
        return list(range(blocks - counts[t], blocks))

    def theirs(t, p):
        return p - counts[t] if splits[t] else p

    loads[0].wait()
    loads[1].wait()
    for k in range(supers):
        part = slice(k * width, (k + 1) * width)
        value = dot(inv[k], rhs[part])
        ly[part] = value
        yb[part] = value.astype(BF)

    def mask(s):
        loads[2 + s].wait()
        cut = slice(s * rows, (s + 1) * rows)
        for k in range(supers):
            part = slice(k * width, (k + 1) * width)
            value = coup[s, part].astype(F32) * pat[k, s].astype(F32)
            mk[part, cut] = value.astype(BF)
            mt[s, :, part] = value.T.astype(BF)

    def share(s, where):
        for first in range(0, len(where), 2):
            two = where[first : first + 2]
            value = dot(mt[s], jnp.concatenate([yb[:, columns[p]] for p in two], axis=1))
            for n, p in enumerate(two):
                yield ancr[s, :, columns[p]] - value[:, n * LANES : (n + 1) * LANES]

    flight = {}

    def offer_urgent(t, p, value):
        n = p - (blocks - counts[t])
        tx[t][n, 0] = value.astype(BF)
        one = pl.ds(0, 1)
        flight[t, p, 0] = copies.start(tx[t].at[n, one], rx[t].at[n, one], across[t])

    def offer_rest(t, p, values):
        if t + 1 == levels:
            return
        n = p - (blocks - counts[t])
        for k, value in enumerate(values):
            tx[t][n, 1 + k] = value.astype(BF)
        later = pl.ds(1, levels - t - 1)
        flight[t, p, 1] = copies.start(tx[t].at[n, later], rx[t].at[n, later], across[t])

    mask(0)
    loads[2 + levels].wait()
    mine = own(0)
    away = [theirs(0, p) for p in mine]
    first_shares = list(share(0, away))
    pl.semaphore_wait(barrier, levels + n_row - 1)
    for p, value in zip(mine, first_shares):
        offer_urgent(0, p, value)
    for p, value in zip(mine, share(0, mine)):
        pend[0, p] = value
    for s in range(1, levels):
        mask(s)
    later_shares = [list(share(s, away)) for s in range(1, levels)]
    for n, p in enumerate(mine):
        offer_rest(0, p, [values[n] for values in later_shares])
    for s in range(1, levels):
        for p, value in zip(mine, share(s, mine)):
            pend[s, p] = value
    loads[3 + levels].wait()

    def turn(k):
        for other in range(n_row):
            cut = slice(other * rows, (other + 1) * rows)
            atr[k, cut] = anc[k, :, cut].T

    later_work = None
    for t in range(levels):
        first_block = block_start(t, levels)
        above = levels - t - 1
        if later_work is not None:
            later_work()
        gathers, to_mate = {}, {}
        for p in own(t):
            n = p - (blocks - counts[t])
            flight[t, p, 0].wait_recv()
            zs[t][n, row] = (pend[t, p] + rx[t][n, 0].astype(F32)).astype(BF)
            spot = zs[t].at[n, row]
            for i in range(1, half):
                other = lax.rem(yy + i, half) * 2 + core
                gathers[p, i] = copies.start(spot, spot, {"row": other})
            to_mate[p] = copies.start(spot, spot, mate)
        for s in range(t + 1, levels):
            turn(first_block + s - t)
        for p in own(t):
            n = p - (blocks - counts[t])

            def sums_of(slot, n=n):
                cut = pl.ds(pl.multiple_of(slot * rows, LANES), rows)
                return [dot(anc[first_block + 1 + k, :, cut], zs[t][n, slot]) for k in range(above)]

            def add(old, new):
                return [a + b for a, b in zip(old, new)]

            total = sums_of(row)
            to_mate[p].wait_recv()
            total = add(total, sums_of(yy * 2 + 1 - core))
            passed = {}
            for i in range(1, half):
                gathers[p, i].wait_recv()
                origin = lax.rem(yy - i + half, half) * 2
                spot = zs[t].at[n, origin + core]
                passed[i] = copies.start(spot, spot, mate)
                total = add(total, sums_of(origin + core))
            for i in range(1, half):
                passed[i].wait_recv()
                origin = lax.rem(yy - i + half, half) * 2
                total = add(total, sums_of(origin + 1 - core))
            if above:
                flight[t, p, 1].wait_recv()
            for k in range(above):
                pend[t + 1 + k, p] = pend[t + 1 + k, p] + rx[t][n, 1 + k].astype(F32) - total[k]
            if above:
                for q in own(t + 1):
                    if theirs(t + 1, q) == p:
                        offer_urgent(t + 1, q, pend[t + 1, p])
                        offer_rest(t + 1, q, [pend[s, p] for s in range(t + 2, levels)])

        def later_work(t=t, first_block=first_block):
            z_all = jnp.concatenate(
                [zs[t][n].reshape(n_row * rows, LANES) for n in range(counts[t])], axis=1
            )
            y_here = dot(anc[first_block], z_all).astype(BF)
            for other in range(n_row):
                acc[t][other] = tdot(anc[first_block, :, other * rows : (other + 1) * rows], y_here)

    later_work()

    arriving = {}

    def need(s, p):
        copy = arriving.pop((s, p), None)
        if copy is not None:
            copy.wait_recv()

    def widen(s, p, t):
        if splits[t]:
            arriving[s, p - counts[t]] = copies.start(
                wide.at[s, p], wide.at[s, p - counts[t]], across[t]
            )

    def leaf_back(first, last, p):
        terms = jnp.concatenate([wide[s, p] for s in range(first, last)], axis=0)
        return ly[:, columns[p]] - dot(mk[:, first * rows : last * rows], terms)

    ring = list(range(1, half)) + [0]
    for t in reversed(range(levels)):
        first_block = block_start(t, levels)
        second, kept = {}, {}
        for p in reversed(own(t)):
            n = p - (blocks - counts[t])
            for s in range(t + 1, levels):
                need(s, p)

            def part_of(dest, p=p, n=n):
                value = acc[t][dest, :, n * LANES : (n + 1) * LANES]
                cut = pl.ds(pl.multiple_of(dest * rows, LANES), rows)
                for s in range(t + 1, levels):
                    value = value - dot(atr[first_block + s - t, cut], wide[s, p])
                return value

            first = {}
            for i in ring:
                dest = lax.rem(yy + i, half) * 2 + 1 - core
                ps[t][n, i] = part_of(dest).astype(BF)
                first[i] = copies.start(ps[t].at[n, i], pr[t].at[n, i], mate)
            for s in range(t + 1, levels):
                widen(s, p, t)
            for i in ring[:-1]:
                dest = lax.rem(yy + i, half) * 2 + core
                value = part_of(dest)
                first[i].wait_recv()
                qs[t][n, i - 1] = (value + pr[t][n, i].astype(F32)).astype(BF)
                second[p, i] = copies.start(
                    qs[t].at[n, i - 1], qr[t].at[n, i - 1], {"row": dest}
                )
            value = part_of(row)
            first[0].wait_recv()
            kept[p] = value + pr[t][n, 0].astype(F32)
            if t == 0 and levels > 1:
                ly[:, columns[p]] = leaf_back(1, levels, p)
        for p in reversed(own(t)):
            n = p - (blocks - counts[t])
            value = kept[p]
            for i in ring[:-1]:
                second[p, i].wait_recv()
                value = value + qr[t][n, i - 1].astype(F32)
            wide[t, p] = value.astype(BF)
            widen(t, p, t)
    for p in reversed(own(0)):
        leaf_out[:, columns[p]] = leaf_back(0, 1, p).astype(BF)
    for p in reversed(range(blocks - counts[0])):
        for s in range(1, levels):
            need(s, p)
        if levels > 1:
            ly[:, columns[p]] = leaf_back(1, levels, p)
    for s in range(levels):
        for p in own(0):
            out[s, :, columns[p]] = wide[s, p]
    for p in reversed(range(blocks - counts[0])):
        need(0, p)
        leaf_out[:, columns[p]] = leaf_back(0, 1, p).astype(BF)
        for s in range(levels):
            out[s, :, columns[p]] = wide[s, p]
    for copy in copies.all:
        copy.wait_send()


def solve(leaf_rhs, leaf_inv, coupling, pattern, anc_rhs, anc):
    levels, rows, cols = anc_rhs.shape
    leaf_rows = leaf_rhs.shape[0]
    supers, width = leaf_inv.shape[:2]
    n_row = lax.axis_size("row")
    half = n_row // 2
    blocks = cols // LANES
    counts, splits = plan(levels, cols)
    span = range(levels)
    less = max(half - 1, 1)
    scratch = [
        pltpu.VMEM(leaf_rhs.shape, BF),
        pltpu.VMEM(leaf_inv.shape, BF),
        pltpu.VMEM(coupling.shape, BF),
        pltpu.VMEM(anc_rhs.shape, F32),
        pltpu.VMEM(anc.shape, BF),
        pltpu.VMEM((leaf_rows, cols), F32),
        pltpu.VMEM((leaf_rows, cols), BF),
        pltpu.VMEM((leaf_rows, levels * rows), BF),
        pltpu.VMEM((levels, rows, leaf_rows), BF),
        pltpu.VMEM((anc.shape[0], n_row * rows, rows), BF),
        pltpu.VMEM((levels, blocks, rows, LANES), F32),
        pltpu.VMEM((levels, blocks, rows, LANES), BF),
    ]
    scratch += [pltpu.VMEM((counts[t], levels - t, rows, LANES), BF) for t in span]
    scratch += [pltpu.VMEM((counts[t], levels - t, rows, LANES), BF) for t in span]
    scratch += [pltpu.VMEM((counts[t], n_row, rows, LANES), BF) for t in span]
    scratch += [pltpu.VMEM((n_row, rows, counts[t] * LANES), F32) for t in span]
    scratch += [pltpu.VMEM((counts[t], half, rows, LANES), BF) for t in span]
    scratch += [pltpu.VMEM((counts[t], half, rows, LANES), BF) for t in span]
    scratch += [pltpu.VMEM((counts[t], less, rows, LANES), BF) for t in span]
    scratch += [pltpu.VMEM((counts[t], less, rows, LANES), BF) for t in span]
    total = copies_needed(levels, n_row, counts, splits)
    scratch += [pltpu.SemaphoreType.DMA((total,)), pltpu.SemaphoreType.DMA((total,))]
    scratch += [pltpu.SemaphoreType.DMA((levels + 4,))]
    away = pl.BlockSpec(memory_space=pl.ANY)
    return pl.pallas_call(
        functools.partial(kernel, (levels, n_row, blocks, supers, width)),
        out_shape=(
            jax.ShapeDtypeStruct((leaf_rows, cols), BF),
            jax.ShapeDtypeStruct((levels, rows, cols), BF),
        ),
        in_specs=[away, away, away, pl.BlockSpec(memory_space=pltpu.SMEM), away, away],
        out_specs=(pl.BlockSpec(memory_space=pltpu.VMEM),) * 2,
        scratch_shapes=scratch,
        compiler_params=pltpu.CompilerParams(collective_id=0, has_side_effects=True),
        name="solve",
    )(leaf_rhs, leaf_inv, coupling, pattern, anc_rhs, anc)


def body(leaf_rhs, leaf_inv, coupling, pattern, anc_rhs, anc_blocks):
    supers, width = leaf_inv.shape[:2]
    leaf_rows, cols = leaf_rhs.shape
    leaf_vb, solved = solve(
        leaf_rhs, leaf_inv, coupling.transpose(1, 0, 2), pattern, anc_rhs[0], anc_blocks[0]
    )
    x_leaf = jnp.einsum(
        "kba,kbr->kar",
        leaf_inv,
        leaf_vb.reshape(supers, width, cols),
        preferred_element_type=F32,
    )
    return (x_leaf.reshape(leaf_rows, cols), solved.astype(F32)[None])


def solution(mesh):
    placed = (
        P(("layer", "row"), None),
        P(("layer", "row"), None, None),
        P(("layer", "row"), None, None),
        P(("layer", "row"), None),
        P("layer", None, "row", None),
        P("layer", None, "row", None),
    )
    return jax.shard_map(
        body,
        mesh=mesh,
        in_specs=placed,
        out_specs=(P(("layer", "row"), None), P("layer", None, "row", None)),
        check_vma=False,
    )
```

```python
import functools

import jax
import jax.numpy as jnp
from jax import lax
from jax.experimental import pallas as pl
from jax.experimental.pallas import tpu as pltpu
from jax.sharding import PartitionSpec as P

MESH = pl.DeviceIdType.MESH
LANES = 128
BF, F32 = jnp.bfloat16, jnp.float32


def block_start(tree_level, level_total):
    return tree_level * level_total - tree_level * (tree_level - 1) // 2


def plan(levels, cols):
    counts, splits, count = [], [], cols // LANES
    for _ in range(levels):
        split = count % 2 == 0
        count = count // 2 if split else count
        counts.append(count)
        splits.append(split)
    return counts, splits


def tdot(a, b):
    return lax.dot_general(a, b, (((0,), (0,)), ((), ())), preferred_element_type=F32)


def dot(a, b):
    return jnp.dot(a, b, preferred_element_type=F32)


class Copies:
    def __init__(self, send, recv):
        self.send, self.recv, self.count, self.all = send, recv, 0, []

    def start(self, src, dst, device):
        copy = pltpu.make_async_remote_copy(
            src_ref=src,
            dst_ref=dst,
            send_sem=self.send.at[self.count],
            recv_sem=self.recv.at[self.count],
            device_id=device,
            device_id_type=MESH,
        )
        copy.start()
        self.count += 1
        self.all.append(copy)
        return copy


def copies_needed(levels, n_row, counts, splits):
    half = n_row // 2
    total = 0
    for t in range(levels):
        each = 2 + 1 + 2 * (half - 1) + half + half - 1
        each += (levels - t) if splits[t] else 0
        total += each * counts[t]
    return total


def kernel(dims, rhs_in, inv_in, coup_in, pat, ancr_in, anc_in, leaf_out, out, *scratch):
    levels, n_row, blocks, supers, width = dims
    rhs, inv, coup, ancr, anc, ly, yb, mk, mt, atr, pend, wide = scratch[:12]
    used = 12
    groups = []
    for _ in range(8):
        groups.append(scratch[used : used + levels])
        used += levels
    tx, rx, zs, acc, ps, pr, qs, qr = groups
    send, recv, local = scratch[used:]
    counts, splits = plan(levels, blocks * LANES)
    rows = anc.shape[1]
    half = n_row // 2
    lay = lax.axis_index("layer")
    row = lax.axis_index("row")
    core = lax.rem(row, 2)
    yy = row // 2
    mate = {"row": yy * 2 + (1 - core)}
    bits = [lax.rem(lay // 2**t, 2) for t in range(levels)]
    across = [{"layer": lay + (1 - 2 * bits[t]) * 2**t} for t in range(levels)]

    loads = []
    for n, (src, dst) in enumerate(
        [(rhs_in, rhs), (inv_in, inv)]
        + [(coup_in.at[s], coup.at[s]) for s in range(levels)]
        + [(ancr_in, ancr), (anc_in, anc)]
    ):
        load = pltpu.make_async_copy(src, dst, local.at[n])
        load.start()
        loads.append(load)

    barrier = pltpu.get_barrier_semaphore()
    for t in range(levels):
        pl.semaphore_signal(barrier, inc=1, device_id=across[t], device_id_type=MESH)
    for i in range(1, n_row):
        pl.semaphore_signal(
            barrier, inc=1, device_id={"row": lax.rem(row + i, n_row)}, device_id_type=MESH
        )
    copies = Copies(send, recv)

    order = list(range(counts[-1]))
    for t in reversed(range(levels)):
        if splits[t]:
            near = [bits[t] * counts[t] + j for j in order]
            order = [(1 - bits[t]) * counts[t] + j for j in order] + near
    columns = [pl.ds(pl.multiple_of(j * LANES, LANES), LANES) for j in order]

    def own(t):
        return list(range(blocks - counts[t], blocks))

    def theirs(t, p):
        return p - counts[t] if splits[t] else p

    loads[0].wait()
    loads[1].wait()
    for k in range(supers):
        part = slice(k * width, (k + 1) * width)
        value = dot(inv[k], rhs[part])
        ly[part] = value
        yb[part] = value.astype(BF)

    def mask(s):
        loads[2 + s].wait()
        cut = slice(s * rows, (s + 1) * rows)
        for k in range(supers):
            part = slice(k * width, (k + 1) * width)
            value = coup[s, part].astype(F32) * pat[s, k].astype(F32)
            mk[part, cut] = value.astype(BF)
            mt[s, :, part] = value.T.astype(BF)

    def share(s, where):
        for first in range(0, len(where), 2):
            two = where[first : first + 2]
            value = dot(mt[s], jnp.concatenate([yb[:, columns[p]] for p in two], axis=1))
            for n, p in enumerate(two):
                yield ancr[s, :, columns[p]] - value[:, n * LANES : (n + 1) * LANES]

    flight = {}

    def offer_urgent(t, p, value):
        n = p - (blocks - counts[t])
        tx[t][n, 0] = value.astype(BF)
        one = pl.ds(0, 1)
        flight[t, p, 0] = copies.start(tx[t].at[n, one], rx[t].at[n, one], across[t])

    def offer_rest(t, p, values):
        if t + 1 == levels:
            return
        n = p - (blocks - counts[t])
        for k, value in enumerate(values):
            tx[t][n, 1 + k] = value.astype(BF)
        later = pl.ds(1, levels - t - 1)
        flight[t, p, 1] = copies.start(tx[t].at[n, later], rx[t].at[n, later], across[t])

    mask(0)
    loads[2 + levels].wait()
    mine = own(0)
    away = [theirs(0, p) for p in mine]
    first_shares = list(share(0, away))
    pl.semaphore_wait(barrier, levels + n_row - 1)
    for p, value in zip(mine, first_shares):
        offer_urgent(0, p, value)
    for p, value in zip(mine, share(0, mine)):
        pend[0, p] = value
    for s in range(1, levels):
        mask(s)
    later_shares = [list(share(s, away)) for s in range(1, levels)]
    for n, p in enumerate(mine):
        offer_rest(0, p, [values[n] for values in later_shares])
    for s in range(1, levels):
        for p, value in zip(mine, share(s, mine)):
            pend[s, p] = value
    loads[3 + levels].wait()

    def turn(k):
        for other in range(n_row):
            cut = slice(other * rows, (other + 1) * rows)
            atr[k, cut] = anc[k, :, cut].T

    later_work, top_y = None, {}
    for t in range(levels):
        first_block = block_start(t, levels)
        above = levels - t - 1
        if later_work is not None:
            later_work()
        gathers, to_mate = {}, {}
        for p in own(t):
            n = p - (blocks - counts[t])
            flight[t, p, 0].wait_recv()
            zs[t][n, row] = (pend[t, p] + rx[t][n, 0].astype(F32)).astype(BF)
            spot = zs[t].at[n, row]
            for i in range(1, half):
                other = lax.rem(yy + i, half) * 2 + core
                gathers[p, i] = copies.start(spot, spot, {"row": other})
            to_mate[p] = copies.start(spot, spot, mate)
        for s in range(t + 1, levels):
            turn(first_block + s - t)
        if not above:
            turn(first_block)
        skip = 1 if above else 0
        for p in own(t):
            n = p - (blocks - counts[t])

            def sums_of(slot, n=n):
                cut = pl.ds(pl.multiple_of(slot * rows, LANES), rows)
                return [
                    dot(anc[first_block + k, :, cut], zs[t][n, slot]) for k in range(skip, above + 1)
                ]

            def add(old, new):
                return [a + b for a, b in zip(old, new)]

            total = sums_of(row)
            to_mate[p].wait_recv()
            total = add(total, sums_of(yy * 2 + 1 - core))
            passed = {}
            for i in range(1, half):
                gathers[p, i].wait_recv()
                origin = lax.rem(yy - i + half, half) * 2
                spot = zs[t].at[n, origin + core]
                passed[i] = copies.start(spot, spot, mate)
                total = add(total, sums_of(origin + core))
            for i in range(1, half):
                passed[i].wait_recv()
                origin = lax.rem(yy - i + half, half) * 2
                total = add(total, sums_of(origin + 1 - core))
            if above:
                flight[t, p, 1].wait_recv()
            else:
                top_y[p] = total[0].astype(BF)
            for k in range(above):
                pend[t + 1 + k, p] = pend[t + 1 + k, p] + rx[t][n, 1 + k].astype(F32) - total[k]
            if above:
                for q in own(t + 1):
                    if theirs(t + 1, q) == p:
                        offer_urgent(t + 1, q, pend[t + 1, p])
                        offer_rest(t + 1, q, [pend[s, p] for s in range(t + 2, levels)])

        def later_work(t=t, first_block=first_block):
            z_all = jnp.concatenate(
                [zs[t][n].reshape(n_row * rows, LANES) for n in range(counts[t])], axis=1
            )
            y_here = dot(anc[first_block], z_all).astype(BF)
            for other in range(n_row):
                acc[t][other] = tdot(anc[first_block, :, other * rows : (other + 1) * rows], y_here)

    arriving = {}

    def need(s, p):
        copy = arriving.pop((s, p), None)
        if copy is not None:
            copy.wait_recv()

    def widen(s, p, t):
        if splits[t]:
            arriving[s, p - counts[t]] = copies.start(
                wide.at[s, p], wide.at[s, p - counts[t]], across[t]
            )

    def leaf_back(first, last, p):
        terms = jnp.concatenate([wide[s, p] for s in range(first, last)], axis=0)
        return ly[:, columns[p]] - dot(mk[:, first * rows : last * rows], terms)

    ring = list(range(1, half)) + [0]
    for t in reversed(range(levels)):
        first_block = block_start(t, levels)
        second, kept = {}, {}
        for p in reversed(own(t)):
            n = p - (blocks - counts[t])
            for s in range(t + 1, levels):
                need(s, p)

            def part_of(dest, p=p, n=n):
                cut = pl.ds(pl.multiple_of(dest * rows, LANES), rows)
                if t + 1 == levels:
                    return dot(atr[first_block, cut], top_y[p])
                value = acc[t][dest, :, n * LANES : (n + 1) * LANES]
                for s in range(t + 1, levels):
                    value = value - dot(atr[first_block + s - t, cut], wide[s, p])
                return value

            first = {}
            for i in ring:
                dest = lax.rem(yy + i, half) * 2 + 1 - core
                ps[t][n, i] = part_of(dest).astype(BF)
                first[i] = copies.start(ps[t].at[n, i], pr[t].at[n, i], mate)
            for s in range(t + 1, levels):
                widen(s, p, t)
            for i in ring[:-1]:
                dest = lax.rem(yy + i, half) * 2 + core
                value = part_of(dest)
                first[i].wait_recv()
                qs[t][n, i - 1] = (value + pr[t][n, i].astype(F32)).astype(BF)
                second[p, i] = copies.start(
                    qs[t].at[n, i - 1], qr[t].at[n, i - 1], {"row": dest}
                )
            value = part_of(row)
            first[0].wait_recv()
            kept[p] = value + pr[t][n, 0].astype(F32)
            if t == 0 and levels > 1 and p != own(t)[0]:
                ly[:, columns[p]] = leaf_back(1, levels, p)
        for p in reversed(own(t)):
            n = p - (blocks - counts[t])
            value = kept[p]
            for i in ring[:-1]:
                second[p, i].wait_recv()
                value = value + qr[t][n, i - 1].astype(F32)
            wide[t, p] = value.astype(BF)
            widen(t, p, t)
            if t == 0 and levels > 1 and p == own(t)[-1]:
                ly[:, columns[own(t)[0]]] = leaf_back(1, levels, own(t)[0])
    for p in reversed(own(0)):
        leaf_out[:, columns[p]] = leaf_back(0, 1, p).astype(BF)
    for p in reversed(range(blocks - counts[0])):
        for s in range(1, levels):
            need(s, p)
        if levels > 1:
            ly[:, columns[p]] = leaf_back(1, levels, p)
    for s in range(levels):
        for p in own(0):
            out[s, :, columns[p]] = wide[s, p]
    for p in reversed(range(blocks - counts[0])):
        need(0, p)
        leaf_out[:, columns[p]] = leaf_back(0, 1, p).astype(BF)
        for s in range(levels):
            out[s, :, columns[p]] = wide[s, p]
    for copy in copies.all:
        copy.wait_send()


def solve(leaf_rhs, leaf_inv, coupling, pattern, anc_rhs, anc):
    levels, rows, cols = anc_rhs.shape
    leaf_rows = leaf_rhs.shape[0]
    supers, width = leaf_inv.shape[:2]
    n_row = lax.axis_size("row")
    half = n_row // 2
    blocks = cols // LANES
    counts, splits = plan(levels, cols)
    span = range(levels)
    less = max(half - 1, 1)
    scratch = [
        pltpu.VMEM(leaf_rhs.shape, BF),
        pltpu.VMEM(leaf_inv.shape, BF),
        pltpu.VMEM(coupling.shape, BF),
        pltpu.VMEM(anc_rhs.shape, F32),
        pltpu.VMEM(anc.shape, BF),
        pltpu.VMEM((leaf_rows, cols), F32),
        pltpu.VMEM((leaf_rows, cols), BF),
        pltpu.VMEM((leaf_rows, levels * rows), BF),
        pltpu.VMEM((levels, rows, leaf_rows), BF),
        pltpu.VMEM((anc.shape[0], n_row * rows, rows), BF),
        pltpu.VMEM((levels, blocks, rows, LANES), F32),
        pltpu.VMEM((levels, blocks, rows, LANES), BF),
    ]
    scratch += [pltpu.VMEM((counts[t], levels - t, rows, LANES), BF) for t in span]
    scratch += [pltpu.VMEM((counts[t], levels - t, rows, LANES), BF) for t in span]
    scratch += [pltpu.VMEM((counts[t], n_row, rows, LANES), BF) for t in span]
    scratch += [pltpu.VMEM((n_row, rows, counts[t] * LANES), F32) for t in span]
    scratch += [pltpu.VMEM((counts[t], half, rows, LANES), BF) for t in span]
    scratch += [pltpu.VMEM((counts[t], half, rows, LANES), BF) for t in span]
    scratch += [pltpu.VMEM((counts[t], less, rows, LANES), BF) for t in span]
    scratch += [pltpu.VMEM((counts[t], less, rows, LANES), BF) for t in span]
    total = copies_needed(levels, n_row, counts, splits)
    scratch += [pltpu.SemaphoreType.DMA((total,)), pltpu.SemaphoreType.DMA((total,))]
    scratch += [pltpu.SemaphoreType.DMA((levels + 4,))]
    away = pl.BlockSpec(memory_space=pl.ANY)
    return pl.pallas_call(
        functools.partial(kernel, (levels, n_row, blocks, supers, width)),
        out_shape=(
            jax.ShapeDtypeStruct((leaf_rows, cols), BF),
            jax.ShapeDtypeStruct((levels, rows, cols), BF),
        ),
        in_specs=[away, away, away, pl.BlockSpec(memory_space=pltpu.SMEM), away, away],
        out_specs=(pl.BlockSpec(memory_space=pltpu.VMEM),) * 2,
        scratch_shapes=scratch,
        compiler_params=pltpu.CompilerParams(collective_id=0, has_side_effects=True),
        name="solve",
    )(leaf_rhs, leaf_inv, coupling, pattern, anc_rhs, anc)


def tail_kernel(inv, vb, solved, x_leaf, x_anc):
    count, width = inv.shape[:2]
    for k in range(count):
        part = slice(k * width, (k + 1) * width)
        x_leaf[part] = tdot(inv[k], vb[part])
    x_anc[...] = solved[...].astype(F32)


def tail(leaf_inv, leaf_vb, solved):
    supers, width = leaf_inv.shape[:2]
    leaf_rows, cols = leaf_vb.shape
    anc_rows = solved.shape[0]
    steps = 4 if supers % 4 == 0 and anc_rows % 64 == 0 else 1
    rows = [leaf_rows // steps, anc_rows // steps]
    flat = [pl.BlockSpec((n, cols), lambda i: (i, 0)) for n in rows]
    return pl.pallas_call(
        tail_kernel,
        grid=(steps,),
        out_shape=(
            jax.ShapeDtypeStruct((leaf_rows, cols), F32),
            jax.ShapeDtypeStruct((anc_rows, cols), F32),
        ),
        in_specs=[pl.BlockSpec((supers // steps, width, width), lambda i: (i, 0, 0))] + flat,
        out_specs=tuple(flat),
        name="tail",
    )(leaf_inv, leaf_vb, solved)


def body(leaf_rhs, leaf_inv, coupling, pattern, anc_rhs, anc_blocks):
    _, levels, rows, cols = anc_rhs.shape
    leaf_vb, solved = solve(
        leaf_rhs, leaf_inv, coupling.transpose(1, 0, 2), pattern.T, anc_rhs[0], anc_blocks[0]
    )
    x_leaf, x_anc = tail(leaf_inv, leaf_vb, solved.reshape(levels * rows, cols))
    return (x_leaf, x_anc.reshape(1, levels, rows, cols))


def solution(mesh):
    placed = (
        P(("layer", "row"), None),
        P(("layer", "row"), None, None),
        P(("layer", "row"), None, None),
        P(("layer", "row"), None),
        P("layer", None, "row", None),
        P("layer", None, "row", None),
    )
    return jax.shard_map(
        body,
        mesh=mesh,
        in_specs=placed,
        out_specs=(P(("layer", "row"), None), P("layer", None, "row", None)),
        check_vma=False,
    )
```

```python
import functools

import jax
import jax.numpy as jnp
from jax import lax
from jax.experimental import pallas as pl
from jax.experimental.pallas import tpu as pltpu
from jax.sharding import PartitionSpec as P

MESH = pl.DeviceIdType.MESH
LANES = 128
BF, F32 = jnp.bfloat16, jnp.float32


def block_start(tree_level, level_total):
    return tree_level * level_total - tree_level * (tree_level - 1) // 2


def plan(levels, cols):
    counts, splits, count = [], [], cols // LANES
    for _ in range(levels):
        split = count % 2 == 0
        count = count // 2 if split else count
        counts.append(count)
        splits.append(split)
    return counts, splits


def tdot(a, b):
    return lax.dot_general(a, b, (((0,), (0,)), ((), ())), preferred_element_type=F32)


def dot(a, b):
    return jnp.dot(a, b, preferred_element_type=F32)


class Copies:
    def __init__(self, send, recv):
        self.send, self.recv, self.count, self.all = send, recv, 0, []

    def start(self, src, dst, device):
        copy = pltpu.make_async_remote_copy(
            src_ref=src,
            dst_ref=dst,
            send_sem=self.send.at[self.count],
            recv_sem=self.recv.at[self.count],
            device_id=device,
            device_id_type=MESH,
        )
        copy.start()
        self.count += 1
        self.all.append(copy)
        return copy


def copies_needed(levels, n_row, counts, splits):
    half = n_row // 2
    total = 0
    for t in range(levels):
        each = 2 + 1 + 2 * (half - 1) + half + half - 1
        each += (levels - t) if splits[t] else 0
        total += each * counts[t]
    return total


def kernel(dims, rhs_in, inv_in, coup_in, pat, ancr_in, anc_in, leaf_out, out, *scratch):
    levels, n_row, blocks, supers, width = dims
    rhs, inv, coup, ancr, anc, ly, yb, mk, mt, atr, pend, wide = scratch[:12]
    used = 12
    groups = []
    for _ in range(8):
        groups.append(scratch[used : used + levels])
        used += levels
    tx, rx, zs, acc, ps, pr, qs, qr = groups
    send, recv, local = scratch[used:]
    counts, splits = plan(levels, blocks * LANES)
    rows = anc.shape[1]
    half = n_row // 2
    lay = lax.axis_index("layer")
    row = lax.axis_index("row")
    core = lax.rem(row, 2)
    yy = row // 2
    mate = {"row": yy * 2 + (1 - core)}
    bits = [lax.rem(lay // 2**t, 2) for t in range(levels)]
    across = [{"layer": lay + (1 - 2 * bits[t]) * 2**t} for t in range(levels)]

    loads = []
    for n, (src, dst) in enumerate(
        [(rhs_in, rhs), (inv_in, inv)]
        + [(coup_in.at[s], coup.at[s]) for s in range(levels)]
        + [(ancr_in, ancr), (anc_in, anc)]
    ):
        load = pltpu.make_async_copy(src, dst, local.at[n])
        load.start()
        loads.append(load)

    barrier = pltpu.get_barrier_semaphore()
    for t in range(levels):
        pl.semaphore_signal(barrier, inc=1, device_id=across[t], device_id_type=MESH)
    for i in range(1, n_row):
        pl.semaphore_signal(
            barrier, inc=1, device_id={"row": lax.rem(row + i, n_row)}, device_id_type=MESH
        )
    copies = Copies(send, recv)

    order = list(range(counts[-1]))
    for t in reversed(range(levels)):
        if splits[t]:
            near = [bits[t] * counts[t] + j for j in order]
            order = [(1 - bits[t]) * counts[t] + j for j in order] + near
    columns = [pl.ds(pl.multiple_of(j * LANES, LANES), LANES) for j in order]

    def own(t):
        return list(range(blocks - counts[t], blocks))

    def theirs(t, p):
        return p - counts[t] if splits[t] else p

    loads[0].wait()
    loads[1].wait()
    for k in range(supers):
        part = slice(k * width, (k + 1) * width)
        value = dot(inv[k], rhs[part])
        ly[part] = value
        yb[part] = value.astype(BF)

    def mask(s):
        loads[2 + s].wait()
        cut = slice(s * rows, (s + 1) * rows)
        for k in range(supers):
            part = slice(k * width, (k + 1) * width)
            value = coup[s, part].astype(F32) * pat[s, k].astype(F32)
            mk[part, cut] = value.astype(BF)
            mt[s, :, part] = value.T.astype(BF)

    def share(s, where):
        for first in range(0, len(where), 2):
            two = where[first : first + 2]
            value = dot(mt[s], jnp.concatenate([yb[:, columns[p]] for p in two], axis=1))
            for n, p in enumerate(two):
                yield ancr[s, :, columns[p]] - value[:, n * LANES : (n + 1) * LANES]

    flight = {}

    def offer_urgent(t, p, value):
        n = p - (blocks - counts[t])
        tx[t][n, 0] = value.astype(BF)
        one = pl.ds(0, 1)
        flight[t, p, 0] = copies.start(tx[t].at[n, one], rx[t].at[n, one], across[t])

    def offer_rest(t, p, values):
        if t + 1 == levels:
            return
        n = p - (blocks - counts[t])
        for k, value in enumerate(values):
            tx[t][n, 1 + k] = value.astype(BF)
        later = pl.ds(1, levels - t - 1)
        flight[t, p, 1] = copies.start(tx[t].at[n, later], rx[t].at[n, later], across[t])

    mask(0)
    loads[2 + levels].wait()
    mine = own(0)
    away = [theirs(0, p) for p in mine]
    first_shares = list(share(0, away))
    pl.semaphore_wait(barrier, levels + n_row - 1)
    for p, value in zip(mine, first_shares):
        offer_urgent(0, p, value)
    for p, value in zip(mine, share(0, mine)):
        pend[0, p] = value
    for s in range(1, levels):
        mask(s)
    later_shares = [list(share(s, away)) for s in range(1, levels)]
    for n, p in enumerate(mine):
        offer_rest(0, p, [values[n] for values in later_shares])
    for s in range(1, levels):
        for p, value in zip(mine, share(s, mine)):
            pend[s, p] = value
    loads[3 + levels].wait()

    def turn(k):
        for other in range(n_row):
            cut = slice(other * rows, (other + 1) * rows)
            atr[k, cut] = anc[k, :, cut].T

    later_work, top_y = None, {}
    for t in range(levels):
        first_block = block_start(t, levels)
        above = levels - t - 1
        if later_work is not None:
            later_work()
        gathers, to_mate = {}, {}
        for p in own(t):
            n = p - (blocks - counts[t])
            flight[t, p, 0].wait_recv()
            zs[t][n, row] = (pend[t, p] + rx[t][n, 0].astype(F32)).astype(BF)
            spot = zs[t].at[n, row]
            for i in range(1, half):
                other = lax.rem(yy + i, half) * 2 + core
                gathers[p, i] = copies.start(spot, spot, {"row": other})
            to_mate[p] = copies.start(spot, spot, mate)
        for s in range(t + 1, levels):
            turn(first_block + s - t)
        if not above:
            turn(first_block)
        skip = 1 if above else 0
        for p in own(t):
            n = p - (blocks - counts[t])

            def sums_of(slot, n=n):
                cut = pl.ds(pl.multiple_of(slot * rows, LANES), rows)
                return [
                    dot(anc[first_block + k, :, cut], zs[t][n, slot]) for k in range(skip, above + 1)
                ]

            def add(old, new):
                return [a + b for a, b in zip(old, new)]

            total = sums_of(row)
            to_mate[p].wait_recv()
            total = add(total, sums_of(yy * 2 + 1 - core))
            passed = {}
            for i in range(1, half):
                gathers[p, i].wait_recv()
                origin = lax.rem(yy - i + half, half) * 2
                spot = zs[t].at[n, origin + core]
                passed[i] = copies.start(spot, spot, mate)
                total = add(total, sums_of(origin + core))
            for i in range(1, half):
                passed[i].wait_recv()
                origin = lax.rem(yy - i + half, half) * 2
                total = add(total, sums_of(origin + 1 - core))
            if above:
                flight[t, p, 1].wait_recv()
            else:
                top_y[p] = total[0].astype(BF)
            for k in range(above):
                pend[t + 1 + k, p] = pend[t + 1 + k, p] + rx[t][n, 1 + k].astype(F32) - total[k]
            if above:
                for q in own(t + 1):
                    if theirs(t + 1, q) == p:
                        offer_urgent(t + 1, q, pend[t + 1, p])
                        offer_rest(t + 1, q, [pend[s, p] for s in range(t + 2, levels)])

        def later_work(t=t, first_block=first_block):
            z_all = jnp.concatenate(
                [zs[t][n].reshape(n_row * rows, LANES) for n in range(counts[t])], axis=1
            )
            y_here = dot(anc[first_block], z_all).astype(BF)
            for other in range(n_row):
                acc[t][other] = tdot(anc[first_block, :, other * rows : (other + 1) * rows], y_here)

    arriving = {}

    def need(s, p):
        copy = arriving.pop((s, p), None)
        if copy is not None:
            copy.wait_recv()

    def widen(s, p, t):
        if splits[t]:
            arriving[s, p - counts[t]] = copies.start(
                wide.at[s, p], wide.at[s, p - counts[t]], across[t]
            )

    def leaf_back(first, last, p):
        terms = jnp.concatenate([wide[s, p] for s in range(first, last)], axis=0)
        return ly[:, columns[p]] - dot(mk[:, first * rows : last * rows], terms)

    ring = list(range(1, half)) + [0]
    for t in reversed(range(levels)):
        first_block = block_start(t, levels)
        second, kept = {}, {}
        for p in reversed(own(t)):
            n = p - (blocks - counts[t])
            for s in range(t + 1, levels):
                need(s, p)

            def part_of(dest, p=p, n=n):
                cut = pl.ds(pl.multiple_of(dest * rows, LANES), rows)
                if t + 1 == levels:
                    return dot(atr[first_block, cut], top_y[p])
                value = acc[t][dest, :, n * LANES : (n + 1) * LANES]
                for s in range(t + 1, levels):
                    value = value - dot(atr[first_block + s - t, cut], wide[s, p])
                return value

            first = {}
            for i in ring:
                dest = lax.rem(yy + i, half) * 2 + 1 - core
                ps[t][n, i] = part_of(dest).astype(BF)
                first[i] = copies.start(ps[t].at[n, i], pr[t].at[n, i], mate)
            for s in range(t + 1, levels):
                widen(s, p, t)
            for i in ring[:-1]:
                dest = lax.rem(yy + i, half) * 2 + core
                value = part_of(dest)
                first[i].wait_recv()
                qs[t][n, i - 1] = (value + pr[t][n, i].astype(F32)).astype(BF)
                second[p, i] = copies.start(
                    qs[t].at[n, i - 1], qr[t].at[n, i - 1], {"row": dest}
                )
            value = part_of(row)
            first[0].wait_recv()
            kept[p] = value + pr[t][n, 0].astype(F32)
            if t == 0 and levels > 1 and p != own(t)[0]:
                ly[:, columns[p]] = leaf_back(1, levels, p)
        for p in reversed(own(t)):
            n = p - (blocks - counts[t])
            value = kept[p]
            for i in ring[:-1]:
                second[p, i].wait_recv()
                value = value + qr[t][n, i - 1].astype(F32)
            wide[t, p] = value.astype(BF)
            widen(t, p, t)
            if t == 0 and levels > 1 and p == own(t)[-1]:
                ly[:, columns[own(t)[0]]] = leaf_back(1, levels, own(t)[0])
    for p in reversed(own(0)):
        leaf_out[:, columns[p]] = leaf_back(0, 1, p).astype(BF)
    for p in reversed(range(blocks - counts[0])):
        for s in range(1, levels):
            need(s, p)
        if levels > 1:
            ly[:, columns[p]] = leaf_back(1, levels, p)
    for s in range(levels):
        for p in own(0):
            out[s, :, columns[p]] = wide[s, p]
    for p in reversed(range(blocks - counts[0])):
        need(0, p)
        leaf_out[:, columns[p]] = leaf_back(0, 1, p).astype(BF)
        for s in range(levels):
            out[s, :, columns[p]] = wide[s, p]
    for copy in copies.all:
        copy.wait_send()


def solve(leaf_rhs, leaf_inv, coupling, pattern, anc_rhs, anc):
    levels, rows, cols = anc_rhs.shape
    leaf_rows = leaf_rhs.shape[0]
    supers, width = leaf_inv.shape[:2]
    n_row = lax.axis_size("row")
    half = n_row // 2
    blocks = cols // LANES
    counts, splits = plan(levels, cols)
    span = range(levels)
    less = max(half - 1, 1)
    scratch = [
        pltpu.VMEM(leaf_rhs.shape, BF),
        pltpu.VMEM(leaf_inv.shape, BF),
        pltpu.VMEM(coupling.shape, BF),
        pltpu.VMEM(anc_rhs.shape, F32),
        pltpu.VMEM(anc.shape, BF),
        pltpu.VMEM((leaf_rows, cols), F32),
        pltpu.VMEM((leaf_rows, cols), BF),
        pltpu.VMEM((leaf_rows, levels * rows), BF),
        pltpu.VMEM((levels, rows, leaf_rows), BF),
        pltpu.VMEM((anc.shape[0], n_row * rows, rows), BF),
        pltpu.VMEM((levels, blocks, rows, LANES), F32),
        pltpu.VMEM((levels, blocks, rows, LANES), BF),
    ]
    scratch += [pltpu.VMEM((counts[t], levels - t, rows, LANES), BF) for t in span]
    scratch += [pltpu.VMEM((counts[t], levels - t, rows, LANES), BF) for t in span]
    scratch += [pltpu.VMEM((counts[t], n_row, rows, LANES), BF) for t in span]
    scratch += [pltpu.VMEM((n_row, rows, counts[t] * LANES), F32) for t in span]
    scratch += [pltpu.VMEM((counts[t], half, rows, LANES), BF) for t in span]
    scratch += [pltpu.VMEM((counts[t], half, rows, LANES), BF) for t in span]
    scratch += [pltpu.VMEM((counts[t], less, rows, LANES), BF) for t in span]
    scratch += [pltpu.VMEM((counts[t], less, rows, LANES), BF) for t in span]
    total = copies_needed(levels, n_row, counts, splits)
    scratch += [pltpu.SemaphoreType.DMA((total,)), pltpu.SemaphoreType.DMA((total,))]
    scratch += [pltpu.SemaphoreType.DMA((levels + 4,))]
    away = pl.BlockSpec(memory_space=pl.ANY)
    return pl.pallas_call(
        functools.partial(kernel, (levels, n_row, blocks, supers, width)),
        out_shape=(
            jax.ShapeDtypeStruct((leaf_rows, cols), BF),
            jax.ShapeDtypeStruct((levels, rows, cols), BF),
        ),
        in_specs=[away, away, away, pl.BlockSpec(memory_space=pltpu.SMEM), away, away],
        out_specs=(pl.BlockSpec(memory_space=pltpu.VMEM),) * 2,
        scratch_shapes=scratch,
        compiler_params=pltpu.CompilerParams(collective_id=0, has_side_effects=True),
        name="solve",
    )(leaf_rhs, leaf_inv, coupling, pattern, anc_rhs, anc)


def tail_kernel(inv, vb, solved, x_leaf, x_anc):
    count, width = inv.shape[:2]
    for k in range(count):
        part = slice(k * width, (k + 1) * width)
        x_leaf[part] = tdot(inv[k], vb[part])
    x_anc[...] = solved[...].astype(F32)


def tail(leaf_inv, leaf_vb, solved):
    supers, width = leaf_inv.shape[:2]
    leaf_rows, cols = leaf_vb.shape
    anc_rows = solved.shape[0]
    steps = 2 if supers % 2 == 0 and anc_rows % 32 == 0 else 1
    rows = [leaf_rows // steps, anc_rows // steps]
    flat = [pl.BlockSpec((n, cols), lambda i: (i, 0)) for n in rows]
    return pl.pallas_call(
        tail_kernel,
        grid=(steps,),
        out_shape=(
            jax.ShapeDtypeStruct((leaf_rows, cols), F32),
            jax.ShapeDtypeStruct((anc_rows, cols), F32),
        ),
        in_specs=[pl.BlockSpec((supers // steps, width, width), lambda i: (i, 0, 0))] + flat,
        out_specs=tuple(flat),
        name="tail",
    )(leaf_inv, leaf_vb, solved)


def body(leaf_rhs, leaf_inv, coupling, pattern, anc_rhs, anc_blocks):
    _, levels, rows, cols = anc_rhs.shape
    leaf_vb, solved = solve(
        leaf_rhs, leaf_inv, coupling.transpose(1, 0, 2), pattern.T, anc_rhs[0], anc_blocks[0]
    )
    x_leaf, x_anc = tail(leaf_inv, leaf_vb, solved.reshape(levels * rows, cols))
    return (x_leaf, x_anc.reshape(1, levels, rows, cols))


def solution(mesh):
    placed = (
        P(("layer", "row"), None),
        P(("layer", "row"), None, None),
        P(("layer", "row"), None, None),
        P(("layer", "row"), None),
        P("layer", None, "row", None),
        P("layer", None, "row", None),
    )
    return jax.shard_map(
        body,
        mesh=mesh,
        in_specs=placed,
        out_specs=(P(("layer", "row"), None), P("layer", None, "row", None)),
        check_vma=False,
    )
```
